256 devices in a mesh: cfg: 2 (over core), tm: 128 (over y, z, x).
Axes of the slice: x: 4, y: 4, z: 8, core: 2. Of those that a mesh axis runs over, the one named last changes fastest.
Arguments:
- queries: bfloat16 [2, 98304, 1152], P('cfg', 'tm'), may hold values from -6 to 6
- key_vectors: bfloat16 [2, 98304, 1152], P('cfg', 'tm'), may hold values from -12 to 12
- value_vectors: bfloat16 [2, 98304, 1152], P('cfg', 'tm'), may hold values from -4 to 4
- out_weight: bfloat16 [1152, 2240], replicated, may hold values from -0.1875 to 0.1875
- first_frame: int32 [256], P('tm'), may hold values from 0 to 255, as said below
Outputs:
- guided: bfloat16 [98304, 2240], P('tm', 'cfg')
The draws below stay inside these ranges and needn't reach their ends.
Inputs may be any that keep to these rules, and one draw needn't show every extreme that they name: first_frame[f] is 0 or lies between f - 4 and f; some frame f has first_frame[f] = f - 4.
All inputs are finite; a program needn't handle non-finite values.
Results may differ from the reference program's by a relative error of at most 0.014.
Values may be sent and summed in bfloat16 or wider, within the bound.
No kernel may reach another device: no remote copies, remote signals or barrier semaphores. Data moves between devices by JAX's collectives and lax.ppermute only.
A program may use at most 192 MiB of HBM per device.

```python
import math
import jax
import jax.numpy as jnp
from jax import lax

D = 2240
H = 36
DH = 32
FR = 2
NEAR = 2
FT = 384
HD = 1152
NF = 256
TOKENS = 98304
WIN = 4


def shared_noise(key):
    noise_key = jax.random.fold_in(key, 11)
    return jnp.clip(jax.random.normal(noise_key, (2, NF, FT, H, DH), jnp.float32), -4.0, 4.0)


def draw_key_vectors(key, part):
    noise = shared_noise(key)
    scale_key = jax.random.fold_in(key, 13)
    lowest = 0.3
    scales = jnp.exp(jax.random.uniform(scale_key, (2, NF, 1, H, DH), jnp.float32, math.log(lowest), math.log(3.0)))
    return (noise * scales).reshape(2, NF * FT, H * DH).astype(jnp.bfloat16)


def draw_value_vectors(key, part):
    noise = shared_noise(key)
    mixing_key = jax.random.fold_in(key, 29)
    own_key = jax.random.fold_in(key, 23)
    offset_key = jax.random.fold_in(key, 27)
    mixing = jax.random.normal(mixing_key, (H, DH, DH), jnp.float32) / math.sqrt(DH)
    mixed = jnp.einsum('bgthd,hde->bgthe', noise, mixing)
    coupled = 0.9 * jnp.clip(mixed, -2.5, 2.5)
    own = 0.3 * jnp.clip(jax.random.normal(own_key, (2, NF, FT, H, DH), jnp.float32), -3.0, 3.0)
    offsets = jax.random.uniform(offset_key, (2, NF, 1, H, DH), jnp.float32, -0.8, 0.8)
    return (coupled + own + offsets).reshape(2, NF * FT, H * DH).astype(jnp.bfloat16)


def draw_first_frame(key, part):
    first_key = jax.random.fold_in(key, 31)
    second_key = jax.random.fold_in(key, 37)
    third_key = jax.random.fold_in(key, 41)
    frame_ids = jnp.arange(NF, dtype=jnp.int32)
    windowed = jax.random.randint(first_key, (NF,), 0, 2, dtype=jnp.int32)
    backward = jax.random.randint(second_key, (NF,), 0, WIN + 1, dtype=jnp.int32)
    starts = jnp.where(windowed == 1, jnp.maximum(frame_ids - backward, 0), 0)
    reaching = (frame_ids % FR == 0) & (frame_ids >= FR) & (frame_ids <= NEAR * FR)
    starts = jnp.where(reaching, 1, starts)
    chosen = jax.random.randint(third_key, (), WIN + 1, NF, dtype=jnp.int32)
    starts = jnp.where(frame_ids == chosen, frame_ids - WIN, starts)
    return starts.astype(jnp.int32)


def shard_levels(rng, dims, shards, low, high):
    factor_of = 1.0
    for dim, shards_of in shards:
        draws = jax.random.uniform(jax.random.fold_in(jax.random.fold_in(rng, 6), dim), (shards_of,), jnp.float32, low / len(shards), high / len(shards))
        factor_of = factor_of * jnp.repeat(jnp.exp(draws), dims[dim] // shards_of).reshape((-1,) + (1,) * (len(dims) - 1 - dim))
    return factor_of


def gaussian(stream_key, dims, spread, limit, split=(), held_as=jnp.bfloat16):
    array = spread * jax.random.normal(stream_key, dims, jnp.float32)
    if split:
        array = array * shard_levels(stream_key, dims, split, -0.22, 0.18)
    return jnp.clip(array, -limit, limit).astype(held_as)


def setup_inputs(seed: int = 0) -> dict:
    keys = jax.random.split(jax.random.key(seed), 6)
    return {
        "queries": gaussian(keys[0], (2, TOKENS, HD), 1.0, 6.0, ((0, 2), (1, 128))),
        "key_vectors": draw_key_vectors(jax.random.fold_in(keys[5], 71), 0),
        "value_vectors": draw_value_vectors(jax.random.fold_in(keys[5], 71), 0),
        "out_weight": gaussian(keys[3], (HD, D), HD ** -0.5, 0.1875),
        "first_frame": draw_first_frame(jax.random.fold_in(keys[5], 71), 0),
    }


guide_scale = 4.5
epsilon = 1e-6


def reference(queries, key_vectors, value_vectors, out_weight, first_frame):
    frame_ids = jnp.arange(NF, dtype=jnp.int32)
    starts = first_frame.astype(jnp.int32)
    results = []
    for branch in range(2):
        query_feats = jnp.maximum(queries[branch], 0).astype(jnp.float32).reshape(NF, FT, H, DH)
        key_feats = jnp.maximum(key_vectors[branch], 0).astype(jnp.float32).reshape(NF, FT, H, DH)
        value_feats = value_vectors[branch].astype(jnp.float32).reshape(NF, FT, H, DH)
        frame_states = jnp.einsum("gthd,gthe->ghde", key_feats, value_feats, precision=lax.Precision.HIGHEST)
        frame_sums = jnp.sum(key_feats, axis=1)
        cumulative_states = jnp.concatenate([jnp.zeros((1, H, DH, DH), jnp.float32), jnp.cumsum(frame_states, axis=0)], axis=0)
        cumulative_sums = jnp.concatenate([jnp.zeros((1, H, DH), jnp.float32), jnp.cumsum(frame_sums, axis=0)], axis=0)
        attended_states = cumulative_states[frame_ids + 1] - cumulative_states[starts]
        attended_sums = cumulative_sums[frame_ids + 1] - cumulative_sums[starts]
        numerator = jnp.einsum("gthd,ghde->gthe", query_feats, attended_states, precision=lax.Precision.HIGHEST)
        denominator = jnp.einsum("gthd,ghd->gth", query_feats, attended_sums, precision=lax.Precision.HIGHEST) + epsilon
        attended = (numerator / denominator[..., None]).astype(jnp.bfloat16).reshape(TOKENS, H * DH)
        results.append(jnp.dot(attended, out_weight, preferred_element_type=jnp.float32))
    return (results[1] + guide_scale * (results[0] - results[1])).astype(jnp.bfloat16)
```

```python
import jax
import jax.numpy as jnp
from jax import lax
from jax.experimental import pallas as pl
from jax.experimental.pallas import tpu as pltpu
from jax.sharding import Mesh
from jax.sharding import PartitionSpec as P

H = 36
DH = 32
FR = 2
FT = 384
HD = H * DH
LANES = 128
BLOCKS = HD // LANES
HEADS_PER_BLOCK = LANES // DH
PACKED = HD + LANES
ROWS = FR * FT
NEAR = 2
TM = ("tm_0", "tm_1", "tm_2")
Y, Z, X = TM
EARLY = ((X, 1), (X, 2), (X, 3), (Z, 1), (Z, 2), (Z, 3), (Z, 4))
LATE = ((Y, 1), (Y, 2), (Y, 3))
VMEM_LIMIT = 16 << 20

guide_scale = 4.5
epsilon = 1e-06


def state_kernel(k_hbm, v_hbm, frames_ref, message_ref, total_ref, k_buf, v_buf, sems):
    chunks = BLOCKS // 3
    width = 3 * LANES

    def copies(c):
        columns = pl.ds(c * width, width)
        return (
            pltpu.make_async_copy(k_hbm.at[:, columns], k_buf.at[:, columns], sems.at[0, c]),
            pltpu.make_async_copy(v_hbm.at[:, columns], v_buf.at[:, columns], sems.at[1, c]),
        )

    for c in range(chunks):
        for copy in copies(c):
            copy.start()
    lane = lax.broadcasted_iota(jnp.int32, (DH, LANES), 1)
    ones = jnp.ones((FT, LANES), jnp.bfloat16)
    sums = [jnp.zeros((DH, LANES), jnp.float32) for _ in range(FR)]
    for c in range(chunks):
        for copy in copies(c):
            copy.wait()
        for b in range(3 * c, 3 * c + 3):
            columns = slice(b * LANES, (b + 1) * LANES)
            states = []
            for f in range(FR):
                rows = slice(f * FT, (f + 1) * FT)
                keys = jnp.maximum(k_buf[rows, columns], 0)
                both = jnp.concatenate([v_buf[rows, columns], ones], axis=1)
                outer = lax.dot_general(
                    keys, both, (((0,), (0,)), ((), ())), preferred_element_type=jnp.float32
                )
                state = jnp.zeros((DH, LANES), jnp.float32)
                for h in range(HEADS_PER_BLOCK):
                    piece = outer[h * DH : (h + 1) * DH]
                    state = jnp.where(lane // DH == h, piece[:, :LANES], state)
                    sums[f] = jnp.where(
                        lane == b * HEADS_PER_BLOCK + h, piece[:, LANES:], sums[f]
                    )
                frames_ref[f, :, columns] = state
                message_ref[f, :, columns] = state.astype(jnp.bfloat16)
                states.append(state)
            total_ref[:, columns] = (states[0] + states[1]).astype(jnp.bfloat16)
    for f in range(FR):
        frames_ref[f, :, HD:] = sums[f]
        message_ref[f, :, HD:] = sums[f].astype(jnp.bfloat16)
    total_ref[:, HD:] = (sums[0] + sums[1]).astype(jnp.bfloat16)


def in_hbm(value):
    return pltpu.with_memory_space_constraint(value, pltpu.HBM)


def frame_states(keys, values):
    return pl.pallas_call(
        state_kernel,
        out_shape=(
            jax.ShapeDtypeStruct((FR, DH, PACKED), jnp.float32),
            jax.ShapeDtypeStruct((FR, DH, PACKED), jnp.bfloat16),
            jax.ShapeDtypeStruct((DH, PACKED), jnp.bfloat16),
        ),
        in_specs=[pl.BlockSpec(memory_space=pltpu.HBM)] * 2,
        out_specs=(pl.BlockSpec(memory_space=pltpu.VMEM),) * 3,
        scratch_shapes=[
            pltpu.VMEM((ROWS, HD), jnp.bfloat16),
            pltpu.VMEM((ROWS, HD), jnp.bfloat16),
            pltpu.SemaphoreType.DMA((2, 3)),
        ],
        compiler_params=pltpu.CompilerParams(vmem_limit_bytes=VMEM_LIMIT),
        cost_estimate=pl.CostEstimate(
            flops=2 * ROWS * HD * 2 * LANES, bytes_accessed=4 * ROWS * HD, transcendentals=0
        ),
        name="frame_states",
    )(in_hbm(keys), in_hbm(values))


def output_kernel(
    q0_hbm, q1_ref, s0_ref, s1_ref, w_hbm, out_hbm,
    q_buf, w_buf, x_buf, out_buf, q_sems, w_sem, out_sems,
):
    width = out_hbm.shape[0]
    part = width // 2

    def q_copy(f):
        rows = pl.ds(f * FT, FT)
        return pltpu.make_async_copy(q0_hbm.at[rows], q_buf.at[rows], q_sems.at[f])

    def out_copy(c):
        rows = pl.ds(c * part, part)
        return pltpu.make_async_copy(out_buf.at[rows], out_hbm.at[rows], out_sems.at[c])

    for f in range(FR):
        q_copy(f).start()
    branch = lax.axis_index("cfg")
    start = pl.multiple_of(branch * width, 8)
    own_scale = jnp.where(branch == 0, guide_scale, 1.0 - guide_scale)
    scales = (own_scale, 1.0 - own_scale)
    w_copy = pltpu.make_async_copy(w_hbm.at[pl.ds(start, width)], w_buf, w_sem)
    w_copy.start()

    head = lax.broadcasted_iota(jnp.int32, (LANES, HD), 0)
    lane = lax.broadcasted_iota(jnp.int32, (LANES, HD), 1)
    spread = (head == lane // DH).astype(jnp.bfloat16)
    row_of = lax.broadcasted_iota(jnp.int32, (LANES, LANES), 0) // DH
    lane_of = lax.broadcasted_iota(jnp.int32, (LANES, LANES), 1) // DH
    own_head = (row_of == lane_of).astype(jnp.bfloat16)
    for f in range(FR):
        rows = slice(f * FT, (f + 1) * FT)
        sums = [
            jnp.dot(s_ref[f, :, HD:], spread, preferred_element_type=jnp.float32).astype(
                jnp.bfloat16
            )
            for s_ref in (s0_ref, s1_ref)
        ]
        q_copy(f).wait()
        for b in range(BLOCKS):
            columns = slice(b * LANES, (b + 1) * LANES)
            mixed = None
            for i, (q_ref, s_ref) in enumerate(((q_buf, s0_ref), (q1_ref, s1_ref))):
                state = jnp.concatenate([s_ref[f, :, columns]] * HEADS_PER_BLOCK, axis=0)
                total = jnp.concatenate([sums[i][:, columns]] * HEADS_PER_BLOCK, axis=0)
                both = jnp.concatenate([state * own_head, total * own_head], axis=1)
                feats = jnp.maximum(q_ref[rows, columns], 0)
                parts = jnp.dot(feats, both, preferred_element_type=jnp.float32)
                attended = parts[:, :LANES] * scales[i] / (parts[:, LANES:] + epsilon)
                mixed = attended if mixed is None else mixed + attended
            x_buf[rows, columns] = mixed.astype(jnp.bfloat16)
    w_copy.wait()
    for c in range(2):
        rows = slice(c * part, (c + 1) * part)
        out_buf[rows, :] = lax.dot_general(
            w_buf[rows, :], x_buf[...], (((1,), (1,)), ((), ())), preferred_element_type=jnp.float32
        ).astype(jnp.bfloat16)
        out_copy(c).start()
    for c in range(2):
        out_copy(c).wait()


def guided_columns(own_queries, other_queries, own_states, other_states, weight):
    width = weight.shape[0] // 2
    hbm = pl.BlockSpec(memory_space=pltpu.HBM)
    vmem = pl.BlockSpec(memory_space=pltpu.VMEM)
    return pl.pallas_call(
        output_kernel,
        out_shape=jax.ShapeDtypeStruct((width, ROWS), jnp.bfloat16),
        in_specs=[hbm, vmem, vmem, vmem, hbm],
        out_specs=hbm,
        scratch_shapes=[
            pltpu.VMEM((ROWS, HD), jnp.bfloat16),
            pltpu.VMEM((width, HD), jnp.bfloat16),
            pltpu.VMEM((ROWS, HD), jnp.bfloat16),
            pltpu.VMEM((width, ROWS), jnp.bfloat16),
            pltpu.SemaphoreType.DMA((FR,)),
            pltpu.SemaphoreType.DMA,
            pltpu.SemaphoreType.DMA((2,)),
        ],
        compiler_params=pltpu.CompilerParams(vmem_limit_bytes=40 << 20),
        cost_estimate=pl.CostEstimate(
            flops=2 * ROWS * HD * (width + 4 * LANES),
            bytes_accessed=2 * (2 * ROWS * HD + HD * width + ROWS * width),
            transcendentals=0,
        ),
        name="guided_columns",
    )(in_hbm(own_queries), other_queries, own_states, other_states, in_hbm(weight))


def comes_before(axis, mask):
    index = lax.axis_index(axis)
    return ((index ^ mask) < index).astype(jnp.float32)


def early_kernel(first_ref, *refs):
    parts, (near1, near2, frames, out_ref) = refs[:-4], refs[-4:]
    device = lax.axis_index(TM)
    before = [comes_before(axis, mask) for axis, mask in EARLY]
    prefix = None
    for part, weight in zip(parts, before, strict=True):
        term = part[...].astype(jnp.float32) * weight
        prefix = term if prefix is None else prefix + term
    for i in range(FR):
        first = first_ref[i]
        value = prefix * (first == 0).astype(jnp.float32)
        for offset, pair in ((1, near1), (2, near2)):
            for j in range(FR):
                source = (device - offset) * FR + j
                reached = ((first != 0) & (first <= source)).astype(jnp.float32)
                value = value + pair[j].astype(jnp.float32) * reached
        for j in range(i + 1):
            reached = (first <= device * FR + j).astype(jnp.float32)
            value = value + frames[j] * reached
        out_ref[i] = value


def late_kernel(first_ref, base_ref, *refs):
    *parts, out_ref = refs
    prefix = None
    for part, (axis, mask) in zip(parts, LATE, strict=True):
        term = part[...].astype(jnp.float32) * comes_before(axis, mask)
        prefix = term if prefix is None else prefix + term
    for i in range(FR):
        whole = (first_ref[i] == 0).astype(jnp.float32)
        out_ref[i] = (base_ref[i] + prefix * whole).astype(jnp.bfloat16)


def small_call(kernel, dtype, name, first_frame, *arrays):
    return pl.pallas_call(
        kernel,
        out_shape=jax.ShapeDtypeStruct((FR, DH, PACKED), dtype),
        in_specs=[pl.BlockSpec(memory_space=pltpu.SMEM)]
        + [pl.BlockSpec(memory_space=pltpu.VMEM)] * len(arrays),
        out_specs=pl.BlockSpec(memory_space=pltpu.VMEM),
        compiler_params=pltpu.CompilerParams(vmem_limit_bytes=4 << 20),
        cost_estimate=pl.CostEstimate(
            flops=4 * DH * PACKED * len(arrays),
            bytes_accessed=4 * DH * PACKED * len(arrays),
            transcendentals=0,
        ),
        name=name,
    )(first_frame, *arrays)


def exchanged(value, axis, mask):
    pairs = [(i, i ^ mask) for i in range(lax.axis_size(axis))]
    return lax.ppermute(value, axis, pairs)


def shifted(value, axis, steps):
    count = lax.axis_size(axis)
    return lax.ppermute(value, axis, [(i, (i + steps) % count) for i in range(count)])


def summed(total, arrived):
    return sum((a.astype(jnp.float32) for a in arrived), total.astype(jnp.float32)).astype(
        jnp.bfloat16
    )


def on_device(queries, key_vectors, value_vectors, out_weight, first_frame):
    own_queries = queries[0]
    other_queries = exchanged(own_queries, "cfg", 1)
    frames, message, total = frame_states(key_vectors[0], value_vectors[0])
    total, other_queries = lax.optimization_barrier((total, other_queries))

    parts_x = [exchanged(total, X, m) for m in (1, 2, 3)]
    total = summed(total, parts_x)
    parts_z = [exchanged(total, Z, m) for m in (1, 2, 3)]
    near = [shifted(message, TM, offset) for offset in range(1, NEAR + 1)]
    total = summed(total, parts_z)
    parts_w = [exchanged(total, Z, 4)]
    total = summed(total, parts_w)
    parts_y = [exchanged(total, Y, m) for m in (1, 2, 3)]

    early = (*parts_x, *parts_z, *parts_w, *near, frames)
    base = small_call(early_kernel, jnp.float32, "early_mix", first_frame, *early)
    own_states = small_call(late_kernel, jnp.bfloat16, "late_mix", first_frame, base, *parts_y)
    other_states = exchanged(own_states, "cfg", 1)
    return guided_columns(
        own_queries, other_queries, own_states, other_states, out_weight.T
    ).T


def solution(mesh):
    torus = Mesh(mesh.devices.reshape(mesh.shape["cfg"], 4, 8, 4), ("cfg", "tm_0", "tm_1", "tm_2"))
    in_specs = (P("cfg", TM, None), P("cfg", TM, None), P("cfg", TM, None), P(), P(TM))
    return jax.shard_map(
        on_device, mesh=torus, in_specs=in_specs, out_specs=P(TM, "cfg"), check_vma=False
    )
```

```python
import jax
import jax.numpy as jnp
from jax import lax
from jax.experimental import pallas as pl
from jax.experimental.pallas import tpu as pltpu
from jax.sharding import Mesh
from jax.sharding import PartitionSpec as P

H = 36
DH = 32
FR = 2
FT = 384
HD = H * DH
LANES = 128
BLOCKS = HD // LANES
HEADS_PER_BLOCK = LANES // DH
PACKED = HD + LANES
ROWS = FR * FT
NEAR = 2
TM = ("tm_0", "tm_1", "tm_2")
Y, Z, X = TM
EARLY = ((X, 1), (X, 2), (X, 3), (Z, 1), (Z, 2), (Z, 3), (Z, 7))
LATE = ((Y, 1), (Y, 2), (Y, 3))
VMEM_LIMIT = 16 << 20

guide_scale = 4.5
epsilon = 1e-06


def state_kernel(k_hbm, v_hbm, frames_ref, message_ref, total_ref, k_buf, v_buf, sems):
    chunks = BLOCKS // 3
    width = 3 * LANES

    def copies(c):
        columns = pl.ds(c * width, width)
        return (
            pltpu.make_async_copy(k_hbm.at[:, columns], k_buf.at[:, columns], sems.at[0, c]),
            pltpu.make_async_copy(v_hbm.at[:, columns], v_buf.at[:, columns], sems.at[1, c]),
        )

    for c in range(chunks):
        for copy in copies(c):
            copy.start()
    lane = lax.broadcasted_iota(jnp.int32, (DH, LANES), 1)
    ones = jnp.ones((FT, LANES), jnp.bfloat16)
    sums = [jnp.zeros((DH, LANES), jnp.float32) for _ in range(FR)]
    for c in range(chunks):
        for copy in copies(c):
            copy.wait()
        for b in range(3 * c, 3 * c + 3):
            columns = slice(b * LANES, (b + 1) * LANES)
            states = []
            for f in range(FR):
                rows = slice(f * FT, (f + 1) * FT)
                keys = jnp.maximum(k_buf[rows, columns], 0)
                both = jnp.concatenate([v_buf[rows, columns], ones], axis=1)
                outer = lax.dot_general(
                    keys, both, (((0,), (0,)), ((), ())), preferred_element_type=jnp.float32
                )
                state = jnp.zeros((DH, LANES), jnp.float32)
                for h in range(HEADS_PER_BLOCK):
                    piece = outer[h * DH : (h + 1) * DH]
                    state = jnp.where(lane // DH == h, piece[:, :LANES], state)
                    sums[f] = jnp.where(
                        lane == b * HEADS_PER_BLOCK + h, piece[:, LANES:], sums[f]
                    )
                frames_ref[f, :, columns] = state
                message_ref[f, :, columns] = state.astype(jnp.bfloat16)
                states.append(state)
            total_ref[:, columns] = (states[0] + states[1]).astype(jnp.bfloat16)
    for f in range(FR):
        frames_ref[f, :, HD:] = sums[f]
        message_ref[f, :, HD:] = sums[f].astype(jnp.bfloat16)
    total_ref[:, HD:] = (sums[0] + sums[1]).astype(jnp.bfloat16)


def in_hbm(value):
    return pltpu.with_memory_space_constraint(value, pltpu.HBM)


def frame_states(keys, values):
    return pl.pallas_call(
        state_kernel,
        out_shape=(
            jax.ShapeDtypeStruct((FR, DH, PACKED), jnp.float32),
            jax.ShapeDtypeStruct((FR, DH, PACKED), jnp.bfloat16),
            jax.ShapeDtypeStruct((DH, PACKED), jnp.bfloat16),
        ),
        in_specs=[pl.BlockSpec(memory_space=pltpu.HBM)] * 2,
        out_specs=(pl.BlockSpec(memory_space=pltpu.VMEM),) * 3,
        scratch_shapes=[
            pltpu.VMEM((ROWS, HD), jnp.bfloat16),
            pltpu.VMEM((ROWS, HD), jnp.bfloat16),
            pltpu.SemaphoreType.DMA((2, 3)),
        ],
        compiler_params=pltpu.CompilerParams(vmem_limit_bytes=VMEM_LIMIT),
        cost_estimate=pl.CostEstimate(
            flops=2 * ROWS * HD * 2 * LANES, bytes_accessed=4 * ROWS * HD, transcendentals=0
        ),
        name="frame_states",
    )(in_hbm(keys), in_hbm(values))


def output_kernel(
    q0_ref, q1_ref, s0_ref, s1_ref, w_ref, out_hbm, x_buf, out_buf, out_sems
):
    width = out_hbm.shape[0]
    part = width // 2

    def out_copy(c):
        rows = pl.ds(c * part, part)
        return pltpu.make_async_copy(out_buf.at[rows], out_hbm.at[rows], out_sems.at[c])

    head = lax.broadcasted_iota(jnp.int32, (LANES, HD), 0)
    lane = lax.broadcasted_iota(jnp.int32, (LANES, HD), 1)
    spread = (head == lane // DH).astype(jnp.bfloat16)
    row_of = lax.broadcasted_iota(jnp.int32, (LANES, LANES), 0) // DH
    lane_of = lax.broadcasted_iota(jnp.int32, (LANES, LANES), 1) // DH
    own_head = (row_of == lane_of).astype(jnp.bfloat16)
    for f in range(FR):
        rows = slice(f * FT, (f + 1) * FT)
        sums = [
            jnp.dot(s_ref[f, :, HD:], spread, preferred_element_type=jnp.float32).astype(
                jnp.bfloat16
            )
            for s_ref in (s0_ref, s1_ref)
        ]
        for b in range(BLOCKS):
            columns = slice(b * LANES, (b + 1) * LANES)
            parts = []
            for i, (q_ref, s_ref) in enumerate(((q0_ref, s0_ref), (q1_ref, s1_ref))):
                state = jnp.concatenate([s_ref[f, :, columns]] * HEADS_PER_BLOCK, axis=0)
                total = jnp.concatenate([sums[i][:, columns]] * HEADS_PER_BLOCK, axis=0)
                both = jnp.concatenate([state * own_head, total * own_head], axis=1)
                feats = jnp.maximum(q_ref[rows, columns], 0)
                parts.append(jnp.dot(feats, both, preferred_element_type=jnp.float32))
            above = [part[:, :LANES] for part in parts]
            below = [part[:, LANES:] + epsilon for part in parts]
            mixed = (above[0] * below[1] + above[1] * below[0]) / (below[0] * below[1])
            x_buf[rows, columns] = mixed.astype(jnp.bfloat16)
    for c in range(2):
        rows = slice(c * part, (c + 1) * part)
        out_buf[rows, :] = lax.dot_general(
            w_ref[rows, :], x_buf[...], (((1,), (1,)), ((), ())), preferred_element_type=jnp.float32
        ).astype(jnp.bfloat16)
        out_copy(c).start()
    for c in range(2):
        out_copy(c).wait()


def fetch_kernel(q_hbm, w_hbm, q_ref, w_ref, sems):
    width = w_ref.shape[0]
    start = pl.multiple_of(lax.axis_index("cfg") * width, 16)
    copies = (
        pltpu.make_async_copy(q_hbm, q_ref, sems.at[0]),
        pltpu.make_async_copy(w_hbm.at[pl.ds(start, width)], w_ref, sems.at[1]),
    )
    for copy in copies:
        copy.start()
    for copy in copies:
        copy.wait()


def fetched(queries, weight):
    width = weight.shape[0] // 2
    return pl.pallas_call(
        fetch_kernel,
        out_shape=(
            jax.ShapeDtypeStruct(queries.shape, queries.dtype),
            jax.ShapeDtypeStruct((width, weight.shape[1]), weight.dtype),
        ),
        in_specs=[pl.BlockSpec(memory_space=pltpu.HBM)] * 2,
        out_specs=(pl.BlockSpec(memory_space=pltpu.VMEM),) * 2,
        scratch_shapes=[pltpu.SemaphoreType.DMA((2,))],
        compiler_params=pltpu.CompilerParams(vmem_limit_bytes=2 << 20),
        cost_estimate=pl.CostEstimate(
            flops=0, bytes_accessed=4 * (queries.size + weight.size // 2), transcendentals=0
        ),
        name="fetch",
    )(in_hbm(queries), in_hbm(weight))


def guided_columns(own_queries, other_queries, own_states, other_states, weight):
    width = weight.shape[0]
    hbm = pl.BlockSpec(memory_space=pltpu.HBM)
    vmem = pl.BlockSpec(memory_space=pltpu.VMEM)
    return pl.pallas_call(
        output_kernel,
        out_shape=jax.ShapeDtypeStruct((width, ROWS), jnp.bfloat16),
        in_specs=[vmem] * 5,
        out_specs=hbm,
        scratch_shapes=[
            pltpu.VMEM((ROWS, HD), jnp.bfloat16),
            pltpu.VMEM((width, ROWS), jnp.bfloat16),
            pltpu.SemaphoreType.DMA((2,)),
        ],
        compiler_params=pltpu.CompilerParams(vmem_limit_bytes=40 << 20),
        cost_estimate=pl.CostEstimate(
            flops=2 * ROWS * HD * (width + 4 * LANES),
            bytes_accessed=2 * (2 * ROWS * HD + HD * width + ROWS * width),
            transcendentals=0,
        ),
        name="guided_columns",
    )(own_queries, other_queries, own_states, other_states, weight)


def comes_before(axis, mask):
    index = lax.axis_index(axis)
    return ((index ^ mask) < index).astype(jnp.float32)


def early_kernel(first_ref, *refs):
    parts, (near1, near2, frames, out_ref) = refs[:-4], refs[-4:]
    device = lax.axis_index(TM)
    before = [comes_before(axis, mask) for axis, mask in EARLY]
    prefix = None
    for part, weight in zip(parts, before, strict=True):
        term = part[...].astype(jnp.float32) * weight
        prefix = term if prefix is None else prefix + term
    for i in range(FR):
        first = first_ref[i]
        value = prefix * (first == 0).astype(jnp.float32)
        for offset, pair in ((1, near1), (2, near2)):
            for j in range(FR):
                source = (device - offset) * FR + j
                reached = ((first != 0) & (first <= source)).astype(jnp.float32)
                value = value + pair[j].astype(jnp.float32) * reached
        for j in range(i + 1):
            reached = (first <= device * FR + j).astype(jnp.float32)
            value = value + frames[j] * reached
        out_ref[i] = value


def late_kernel(first_ref, base_ref, *refs):
    *parts, out_ref = refs
    prefix = None
    for part, (axis, mask) in zip(parts, LATE, strict=True):
        term = part[...].astype(jnp.float32) * comes_before(axis, mask)
        prefix = term if prefix is None else prefix + term
    own_scale = jnp.where(lax.axis_index("cfg") == 0, guide_scale, 1.0 - guide_scale)
    for i in range(FR):
        whole = (first_ref[i] == 0).astype(jnp.float32)
        value = base_ref[i] + prefix * whole
        out_ref[i, :, :HD] = (value[:, :HD] * own_scale).astype(jnp.bfloat16)
        out_ref[i, :, HD:] = value[:, HD:].astype(jnp.bfloat16)


def small_call(kernel, dtype, name, first_frame, *arrays):
    return pl.pallas_call(
        kernel,
        out_shape=jax.ShapeDtypeStruct((FR, DH, PACKED), dtype),
        in_specs=[pl.BlockSpec(memory_space=pltpu.SMEM)]
        + [pl.BlockSpec(memory_space=pltpu.VMEM)] * len(arrays),
        out_specs=pl.BlockSpec(memory_space=pltpu.VMEM),
        compiler_params=pltpu.CompilerParams(vmem_limit_bytes=4 << 20),
        cost_estimate=pl.CostEstimate(
            flops=4 * DH * PACKED * len(arrays),
            bytes_accessed=4 * DH * PACKED * len(arrays),
            transcendentals=0,
        ),
        name=name,
    )(first_frame, *arrays)


def exchanged(value, axis, mask):
    pairs = [(i, i ^ mask) for i in range(lax.axis_size(axis))]
    return lax.ppermute(value, axis, pairs)


def shifted(value, axis, steps):
    count = lax.axis_size(axis)
    return lax.ppermute(value, axis, [(i, (i + steps) % count) for i in range(count)])


def summed(total, arrived):
    return sum((a.astype(jnp.float32) for a in arrived), total.astype(jnp.float32)).astype(
        jnp.bfloat16
    )


def on_device(queries, key_vectors, value_vectors, out_weight, first_frame):
    own_queries = queries[0]
    other_queries = exchanged(own_queries, "cfg", 1)
    frames, message, total = frame_states(key_vectors[0], value_vectors[0])
    total, other_queries = lax.optimization_barrier((total, other_queries))

    parts_x = [exchanged(total, X, m) for m in (1, 2, 3)]
    total = summed(total, parts_x)
    total, later_queries, later_weight = lax.optimization_barrier((total, own_queries, out_weight.T))
    held_queries, half_weight = fetched(later_queries, later_weight)
    parts_z = [exchanged(total, Z, m) for m in (1, 2, 3)]
    near = [shifted(message, TM, offset) for offset in range(1, NEAR + 1)]
    total = summed(total, parts_z)
    total, held_queries, half_weight = lax.optimization_barrier((total, held_queries, half_weight))
    parts_w = [exchanged(total, Z, 7)]
    total = summed(total, parts_w)
    parts_y = [exchanged(total, Y, m) for m in (1, 2, 3)]

    early = (*parts_x, *parts_z, *parts_w, *near, frames)
    base = small_call(early_kernel, jnp.float32, "early_mix", first_frame, *early)
    own_states = small_call(late_kernel, jnp.bfloat16, "late_mix", first_frame, base, *parts_y)
    other_states = exchanged(own_states, "cfg", 1)
    return guided_columns(
        held_queries, other_queries, own_states, other_states, half_weight
    ).T


def solution(mesh):
    torus = Mesh(mesh.devices.reshape(mesh.shape["cfg"], 4, 8, 4), ("cfg", "tm_0", "tm_1", "tm_2"))
    in_specs = (P("cfg", TM, None), P("cfg", TM, None), P("cfg", TM, None), P(), P(TM))
    return jax.shard_map(
        on_device, mesh=torus, in_specs=in_specs, out_specs=P(TM, "cfg"), check_vma=False
    )
```

```python
import jax
import jax.numpy as jnp
from jax import lax
from jax.experimental import pallas as pl
from jax.experimental.pallas import tpu as pltpu
from jax.sharding import Mesh
from jax.sharding import PartitionSpec as P

H = 36
DH = 32
FR = 2
FT = 384
HD = H * DH
LANES = 128
BLOCKS = HD // LANES
HEADS_PER_BLOCK = LANES // DH
PACKED = HD + LANES
ROWS = FR * FT
TM = ("tm_0", "tm_1", "tm_2")
Y, Z, X = TM
ROW = (Y, Z)
MASKS = (1, 2, 3)
EARLY = ((Z, 1), (Z, 2), (Z, 3), (Z, 7))
LATE = ((Y, 1), (Y, 2), (Y, 3))
VMEM_LIMIT = 16 << 20

guide_scale = 4.5
epsilon = 1e-06


def state_kernel(k_hbm, v_hbm, frames_ref, total_ref, second_ref, k_buf, v_buf, sems):
    chunks = BLOCKS // 3
    width = 3 * LANES

    def copies(c):
        columns = pl.ds(c * width, width)
        return (
            pltpu.make_async_copy(k_hbm.at[:, columns], k_buf.at[:, columns], sems.at[0, c]),
            pltpu.make_async_copy(v_hbm.at[:, columns], v_buf.at[:, columns], sems.at[1, c]),
        )

    for c in range(chunks):
        for copy in copies(c):
            copy.start()
    lane = lax.broadcasted_iota(jnp.int32, (DH, LANES), 1)
    ones = jnp.ones((FT, LANES), jnp.bfloat16)
    sums = [jnp.zeros((DH, LANES), jnp.float32) for _ in range(FR)]
    for c in range(chunks):
        for copy in copies(c):
            copy.wait()
        for b in range(3 * c, 3 * c + 3):
            columns = slice(b * LANES, (b + 1) * LANES)
            states = []
            for f in range(FR):
                rows = slice(f * FT, (f + 1) * FT)
                keys = jnp.maximum(k_buf[rows, columns], 0)
                both = jnp.concatenate([v_buf[rows, columns], ones], axis=1)
                outer = lax.dot_general(
                    keys, both, (((0,), (0,)), ((), ())), preferred_element_type=jnp.float32
                )
                state = jnp.zeros((DH, LANES), jnp.float32)
                for h in range(HEADS_PER_BLOCK):
                    piece = outer[h * DH : (h + 1) * DH]
                    state = jnp.where(lane // DH == h, piece[:, :LANES], state)
                    sums[f] = jnp.where(
                        lane == b * HEADS_PER_BLOCK + h, piece[:, LANES:], sums[f]
                    )
                frames_ref[f, :, columns] = state
                states.append(state)
            total_ref[:, columns] = (states[0] + states[1]).astype(jnp.bfloat16)
            second_ref[:, columns] = states[1].astype(jnp.bfloat16)
    for f in range(FR):
        frames_ref[f, :, HD:] = sums[f]
    total_ref[:, HD:] = (sums[0] + sums[1]).astype(jnp.bfloat16)
    second_ref[:, HD:] = sums[1].astype(jnp.bfloat16)


def in_hbm(value):
    return pltpu.with_memory_space_constraint(value, pltpu.HBM)


def frame_states(keys, values):
    return pl.pallas_call(
        state_kernel,
        out_shape=(
            jax.ShapeDtypeStruct((FR, DH, PACKED), jnp.float32),
            jax.ShapeDtypeStruct((DH, PACKED), jnp.bfloat16),
            jax.ShapeDtypeStruct((DH, PACKED), jnp.bfloat16),
        ),
        in_specs=[pl.BlockSpec(memory_space=pltpu.HBM)] * 2,
        out_specs=(pl.BlockSpec(memory_space=pltpu.VMEM),) * 3,
        scratch_shapes=[
            pltpu.VMEM((ROWS, HD), jnp.bfloat16),
            pltpu.VMEM((ROWS, HD), jnp.bfloat16),
            pltpu.SemaphoreType.DMA((2, 3)),
        ],
        compiler_params=pltpu.CompilerParams(vmem_limit_bytes=VMEM_LIMIT),
        cost_estimate=pl.CostEstimate(
            flops=2 * ROWS * HD * 2 * LANES, bytes_accessed=4 * ROWS * HD, transcendentals=0
        ),
        name="frame_states",
    )(in_hbm(keys), in_hbm(values))


def output_kernel(
    q0_ref, q1_ref, s0_ref, s1_ref, w_ref, out_hbm, x_buf, out_buf, out_sems
):
    width = out_hbm.shape[0]
    part = width // 2

    def out_copy(c):
        rows = pl.ds(c * part, part)
        return pltpu.make_async_copy(out_buf.at[rows], out_hbm.at[rows], out_sems.at[c])

    head = lax.broadcasted_iota(jnp.int32, (LANES, HD), 0)
    lane = lax.broadcasted_iota(jnp.int32, (LANES, HD), 1)
    spread = (head == lane // DH).astype(jnp.bfloat16)
    row_of = lax.broadcasted_iota(jnp.int32, (LANES, LANES), 0) // DH
    lane_of = lax.broadcasted_iota(jnp.int32, (LANES, LANES), 1) // DH
    own_head = (row_of == lane_of).astype(jnp.bfloat16)
    for f in range(FR):
        rows = slice(f * FT, (f + 1) * FT)
        sums = [
            jnp.dot(s_ref[f, :, HD:], spread, preferred_element_type=jnp.float32).astype(
                jnp.bfloat16
            )
            for s_ref in (s0_ref, s1_ref)
        ]
        for b in range(BLOCKS):
            columns = slice(b * LANES, (b + 1) * LANES)
            parts = []
            for i, (q_ref, s_ref) in enumerate(((q0_ref, s0_ref), (q1_ref, s1_ref))):
                state = jnp.concatenate([s_ref[f, :, columns]] * HEADS_PER_BLOCK, axis=0)
                total = jnp.concatenate([sums[i][:, columns]] * HEADS_PER_BLOCK, axis=0)
                both = jnp.concatenate([state * own_head, total * own_head], axis=1)
                feats = jnp.maximum(q_ref[rows, columns], 0)
                parts.append(jnp.dot(feats, both, preferred_element_type=jnp.float32))
            above = [part[:, :LANES] for part in parts]
            below = [part[:, LANES:] + epsilon for part in parts]
            mixed = (above[0] * below[1] + above[1] * below[0]) / (below[0] * below[1])
            x_buf[rows, columns] = mixed.astype(jnp.bfloat16)
    for c in range(2):
        rows = slice(c * part, (c + 1) * part)
        out_buf[rows, :] = lax.dot_general(
            w_ref[rows, :], x_buf[...], (((1,), (1,)), ((), ())), preferred_element_type=jnp.float32
        ).astype(jnp.bfloat16)
        out_copy(c).start()
    for c in range(2):
        out_copy(c).wait()


def fetch_kernel(q_hbm, w_hbm, q_ref, w_ref, sems):
    width = w_ref.shape[0]
    start = pl.multiple_of(lax.axis_index("cfg") * width, 16)
    copies = (
        pltpu.make_async_copy(q_hbm, q_ref, sems.at[0]),
        pltpu.make_async_copy(w_hbm.at[pl.ds(start, width)], w_ref, sems.at[1]),
    )
    for copy in copies:
        copy.start()
    for copy in copies:
        copy.wait()


def fetched(queries, weight):
    width = weight.shape[0] // 2
    return pl.pallas_call(
        fetch_kernel,
        out_shape=(
            jax.ShapeDtypeStruct(queries.shape, queries.dtype),
            jax.ShapeDtypeStruct((width, weight.shape[1]), weight.dtype),
        ),
        in_specs=[pl.BlockSpec(memory_space=pltpu.HBM)] * 2,
        out_specs=(pl.BlockSpec(memory_space=pltpu.VMEM),) * 2,
        scratch_shapes=[pltpu.SemaphoreType.DMA((2,))],
        compiler_params=pltpu.CompilerParams(vmem_limit_bytes=2 << 20),
        cost_estimate=pl.CostEstimate(
            flops=0, bytes_accessed=4 * (queries.size + weight.size // 2), transcendentals=0
        ),
        name="fetch",
    )(in_hbm(queries), in_hbm(weight))


def guided_columns(own_queries, other_queries, own_states, other_states, weight):
    width = weight.shape[0]
    hbm = pl.BlockSpec(memory_space=pltpu.HBM)
    vmem = pl.BlockSpec(memory_space=pltpu.VMEM)
    return pl.pallas_call(
        output_kernel,
        out_shape=jax.ShapeDtypeStruct((width, ROWS), jnp.bfloat16),
        in_specs=[vmem] * 5,
        out_specs=hbm,
        scratch_shapes=[
            pltpu.VMEM((ROWS, HD), jnp.bfloat16),
            pltpu.VMEM((width, ROWS), jnp.bfloat16),
            pltpu.SemaphoreType.DMA((2,)),
        ],
        compiler_params=pltpu.CompilerParams(vmem_limit_bytes=40 << 20),
        cost_estimate=pl.CostEstimate(
            flops=2 * ROWS * HD * (width + 4 * LANES),
            bytes_accessed=2 * (2 * ROWS * HD + HD * width + ROWS * width),
            transcendentals=0,
        ),
        name="guided_columns",
    )(own_queries, other_queries, own_states, other_states, weight)


def comes_before(axis, mask):
    index = lax.axis_index(axis)
    return ((index ^ mask) < index).astype(jnp.float32)


def row_source(mask, j):
    x = lax.axis_index(X)
    return (lax.axis_index(TM) - x + (x ^ mask)) * FR + j


def reached_part(first, mask, both, second):
    one = (first <= row_source(mask, 1)).astype(jnp.float32)
    two = (first <= row_source(mask, 0)).astype(jnp.float32)
    return both.astype(jnp.float32) * two + second.astype(jnp.float32) * (one - two)


def window_kernel(first_ref, total1, total2, total3, second1, second2, second3, frames, out_ref):
    others = tuple(zip(MASKS, (total1, total2, total3), (second1, second2, second3), strict=True))
    for i in range(FR):
        first = first_ref[i]
        value = reached_part(first, 0, frames[0] + frames[1], frames[1])
        for mask, both, second in others:
            value = value + reached_part(first, mask, both[...], second[...])
        out_ref[i] = (value * (first != 0).astype(jnp.float32)).astype(jnp.bfloat16)


def early_kernel(first_ref, *refs):
    parts, refs = refs[: len(EARLY)], refs[len(EARLY) :]
    totals, seconds, (window, frames, out_ref) = refs[:3], refs[3:6], refs[6:]
    prefix = None
    for part, (axis, mask) in zip(parts, EARLY, strict=True):
        term = part[...].astype(jnp.float32) * comes_before(axis, mask)
        prefix = term if prefix is None else prefix + term
    later_row = (lax.axis_index(ROW) > 0).astype(jnp.float32)
    for i in range(FR):
        first = first_ref[i]
        value = prefix * (first == 0).astype(jnp.float32)
        value = value + window[i].astype(jnp.float32) * later_row
        for mask, both, second in zip(MASKS, totals, seconds, strict=True):
            part = reached_part(first, mask, both[...], second[...])
            value = value + part * comes_before(X, mask)
        for j in range(i + 1):
            value = value + frames[j] * (first <= row_source(0, j)).astype(jnp.float32)
        out_ref[i] = value


def late_kernel(first_ref, base_ref, *refs):
    *parts, out_ref = refs
    prefix = None
    for part, (axis, mask) in zip(parts, LATE, strict=True):
        term = part[...].astype(jnp.float32) * comes_before(axis, mask)
        prefix = term if prefix is None else prefix + term
    own_scale = jnp.where(lax.axis_index("cfg") == 0, guide_scale, 1.0 - guide_scale)
    for i in range(FR):
        whole = (first_ref[i] == 0).astype(jnp.float32)
        value = base_ref[i] + prefix * whole
        out_ref[i, :, :HD] = (value[:, :HD] * own_scale).astype(jnp.bfloat16)
        out_ref[i, :, HD:] = value[:, HD:].astype(jnp.bfloat16)


def small_call(kernel, dtype, name, first_frame, *arrays):
    return pl.pallas_call(
        kernel,
        out_shape=jax.ShapeDtypeStruct((FR, DH, PACKED), dtype),
        in_specs=[pl.BlockSpec(memory_space=pltpu.SMEM)]
        + [pl.BlockSpec(memory_space=pltpu.VMEM)] * len(arrays),
        out_specs=pl.BlockSpec(memory_space=pltpu.VMEM),
        compiler_params=pltpu.CompilerParams(vmem_limit_bytes=4 << 20),
        cost_estimate=pl.CostEstimate(
            flops=4 * DH * PACKED * len(arrays),
            bytes_accessed=4 * DH * PACKED * len(arrays),
            transcendentals=0,
        ),
        name=name,
    )(first_frame, *arrays)


def exchanged(value, axis, mask):
    pairs = [(i, i ^ mask) for i in range(lax.axis_size(axis))]
    return lax.ppermute(value, axis, pairs)


def shifted(value, axis, steps):
    count = lax.axis_size(axis)
    return lax.ppermute(value, axis, [(i, (i + steps) % count) for i in range(count)])


def summed(total, arrived):
    return sum((a.astype(jnp.float32) for a in arrived), total.astype(jnp.float32)).astype(
        jnp.bfloat16
    )


def on_device(queries, key_vectors, value_vectors, out_weight, first_frame):
    own_queries = queries[0]
    other_queries = exchanged(own_queries, "cfg", 1)
    next_first = shifted(first_frame, ROW, -1)
    frames, total, second = frame_states(key_vectors[0], value_vectors[0])

    parts_x = [exchanged(total, X, m) for m in MASKS]
    total = summed(total, parts_x)
    total, other_queries, next_first = lax.optimization_barrier((total, other_queries, next_first))
    seconds = [exchanged(second, X, m) for m in MASKS]
    total, later_queries, later_weight = lax.optimization_barrier((total, own_queries, out_weight.T))
    held_queries, half_weight = fetched(later_queries, later_weight)
    parts_z = [exchanged(total, Z, m) for m in (1, 2, 3)]
    window = small_call(
        window_kernel, jnp.bfloat16, "window_mix", next_first, *parts_x, *seconds, frames
    )
    window = shifted(window, ROW, 1)
    total = summed(total, parts_z)
    total, held_queries, half_weight = lax.optimization_barrier((total, held_queries, half_weight))
    parts_w = [exchanged(total, Z, 7)]
    total = summed(total, parts_w)
    parts_y = [exchanged(total, Y, m) for m in (1, 2, 3)]

    early = (*parts_z, *parts_w, *parts_x, *seconds, window, frames)
    base = small_call(early_kernel, jnp.float32, "early_mix", first_frame, *early)
    own_states = small_call(late_kernel, jnp.bfloat16, "late_mix", first_frame, base, *parts_y)
    other_states = exchanged(own_states, "cfg", 1)
    return guided_columns(
        held_queries, other_queries, own_states, other_states, half_weight
    ).T


def solution(mesh):
    torus = Mesh(mesh.devices.reshape(mesh.shape["cfg"], 4, 8, 4), ("cfg", "tm_0", "tm_1", "tm_2"))
    in_specs = (P("cfg", TM, None), P("cfg", TM, None), P("cfg", TM, None), P(), P(TM))
    return jax.shard_map(
        on_device, mesh=torus, in_specs=in_specs, out_specs=P(TM, "cfg"), check_vma=False
    )
```

```python
import jax
import jax.numpy as jnp
from jax import lax
from jax.experimental import pallas as pl
from jax.experimental.pallas import tpu as pltpu
from jax.sharding import Mesh
from jax.sharding import PartitionSpec as P

H = 36
DH = 32
FR = 2
FT = 384
HD = H * DH
LANES = 128
BLOCKS = HD // LANES
HEADS_PER_BLOCK = LANES // DH
PACKED = HD + LANES
ROWS = FR * FT
TM = ("tm_0", "tm_1", "tm_2")
Y, Z, X = TM
ROW = (Y, Z)
MASKS = (1, 2, 3)
EARLY = ((Z, 1), (Z, 2), (Z, 3), (Z, 7))
LATE = ((Y, 1), (Y, 2), (Y, 3))
VMEM_LIMIT = 16 << 20

guide_scale = 4.5
epsilon = 1e-06


def state_kernel(k_hbm, v_hbm, frames_ref, total_ref, second_ref, k_buf, v_buf, sems):
    def copies(f):
        rows = pl.ds(f * FT, FT)
        return (
            pltpu.make_async_copy(k_hbm.at[rows], k_buf.at[rows], sems.at[0, f]),
            pltpu.make_async_copy(v_hbm.at[rows], v_buf.at[rows], sems.at[1, f]),
        )

    for f in range(FR):
        for copy in copies(f):
            copy.start()
    lane = lax.broadcasted_iota(jnp.int32, (DH, LANES), 1)
    ones = jnp.ones((FT, LANES), jnp.bfloat16)
    for f in range(FR):
        rows = slice(f * FT, (f + 1) * FT)
        for copy in copies(f):
            copy.wait()
        sums = jnp.zeros((DH, LANES), jnp.float32)
        for b in range(BLOCKS):
            columns = slice(b * LANES, (b + 1) * LANES)
            keys = jnp.maximum(k_buf[rows, columns], 0)
            both = jnp.concatenate([v_buf[rows, columns], ones], axis=1)
            outer = lax.dot_general(
                keys, both, (((0,), (0,)), ((), ())), preferred_element_type=jnp.float32
            )
            state = jnp.zeros((DH, LANES), jnp.float32)
            for h in range(HEADS_PER_BLOCK):
                piece = outer[h * DH : (h + 1) * DH]
                state = jnp.where(lane // DH == h, piece[:, :LANES], state)
                sums = jnp.where(lane == b * HEADS_PER_BLOCK + h, piece[:, LANES:], sums)
            frames_ref[f, :, columns] = state
        frames_ref[f, :, HD:] = sums
    second = frames_ref[FR - 1]
    second_ref[...] = second.astype(jnp.bfloat16)
    total_ref[...] = (frames_ref[0] + second).astype(jnp.bfloat16)


def in_hbm(value):
    return pltpu.with_memory_space_constraint(value, pltpu.HBM)


def frame_states(keys, values):
    return pl.pallas_call(
        state_kernel,
        out_shape=(
            jax.ShapeDtypeStruct((FR, DH, PACKED), jnp.float32),
            jax.ShapeDtypeStruct((DH, PACKED), jnp.bfloat16),
            jax.ShapeDtypeStruct((DH, PACKED), jnp.bfloat16),
        ),
        in_specs=[pl.BlockSpec(memory_space=pltpu.HBM)] * 2,
        out_specs=(pl.BlockSpec(memory_space=pltpu.VMEM),) * 3,
        scratch_shapes=[
            pltpu.VMEM((ROWS, HD), jnp.bfloat16),
            pltpu.VMEM((ROWS, HD), jnp.bfloat16),
            pltpu.SemaphoreType.DMA((2, FR)),
        ],
        compiler_params=pltpu.CompilerParams(vmem_limit_bytes=VMEM_LIMIT),
        cost_estimate=pl.CostEstimate(
            flops=2 * ROWS * HD * 2 * LANES, bytes_accessed=4 * ROWS * HD, transcendentals=0
        ),
        name="frame_states",
    )(in_hbm(keys), in_hbm(values))


def output_kernel(
    q0_ref, q1_ref, s0_ref, s1_ref, w_ref, out_hbm, x_buf, out_buf, out_sems
):
    width = out_hbm.shape[0]
    part = width // 2

    def out_copy(c):
        rows = pl.ds(c * part, part)
        return pltpu.make_async_copy(out_buf.at[rows], out_hbm.at[rows], out_sems.at[c])

    head = lax.broadcasted_iota(jnp.int32, (LANES, HD), 0)
    lane = lax.broadcasted_iota(jnp.int32, (LANES, HD), 1)
    spread = (head == lane // DH).astype(jnp.bfloat16)
    row_of = lax.broadcasted_iota(jnp.int32, (LANES, LANES), 0) // DH
    lane_of = lax.broadcasted_iota(jnp.int32, (LANES, LANES), 1) // DH
    own_head = (row_of == lane_of).astype(jnp.bfloat16)
    for f in range(FR):
        rows = slice(f * FT, (f + 1) * FT)
        sums = [
            jnp.dot(s_ref[f, :, HD:], spread, preferred_element_type=jnp.float32).astype(
                jnp.bfloat16
            )
            for s_ref in (s0_ref, s1_ref)
        ]
        for b in range(BLOCKS):
            columns = slice(b * LANES, (b + 1) * LANES)
            parts = []
            for i, (q_ref, s_ref) in enumerate(((q0_ref, s0_ref), (q1_ref, s1_ref))):
                state = jnp.concatenate([s_ref[f, :, columns]] * HEADS_PER_BLOCK, axis=0)
                total = jnp.concatenate([sums[i][:, columns]] * HEADS_PER_BLOCK, axis=0)
                both = jnp.concatenate([state * own_head, total * own_head], axis=1)
                feats = jnp.maximum(q_ref[rows, columns], 0)
                parts.append(jnp.dot(feats, both, preferred_element_type=jnp.float32))
            above = [part[:, :LANES] for part in parts]
            below = [part[:, LANES:] + epsilon for part in parts]
            mixed = (above[0] * below[1] + above[1] * below[0]) / (below[0] * below[1])
            x_buf[rows, columns] = mixed.astype(jnp.bfloat16)
    for c in range(2):
        rows = slice(c * part, (c + 1) * part)
        out_buf[rows, :] = lax.dot_general(
            w_ref[rows, :], x_buf[...], (((1,), (1,)), ((), ())), preferred_element_type=jnp.float32
        ).astype(jnp.bfloat16)
        out_copy(c).start()
    for c in range(2):
        out_copy(c).wait()


def fetch_kernel(w_hbm, w_ref, sem):
    width = w_ref.shape[0]
    start = pl.multiple_of(lax.axis_index("cfg") * width, 16)
    copy = pltpu.make_async_copy(w_hbm.at[pl.ds(start, width)], w_ref, sem)
    copy.start()
    copy.wait()


def fetched(weight):
    width = weight.shape[0] // 2
    return pl.pallas_call(
        fetch_kernel,
        out_shape=jax.ShapeDtypeStruct((width, weight.shape[1]), weight.dtype),
        in_specs=[pl.BlockSpec(memory_space=pltpu.HBM)],
        out_specs=pl.BlockSpec(memory_space=pltpu.VMEM),
        scratch_shapes=[pltpu.SemaphoreType.DMA],
        compiler_params=pltpu.CompilerParams(vmem_limit_bytes=2 << 20),
        cost_estimate=pl.CostEstimate(
            flops=0, bytes_accessed=2 * weight.size, transcendentals=0
        ),
        name="fetch",
    )(in_hbm(weight))


def guided_columns(own_queries, other_queries, own_states, other_states, weight):
    width = weight.shape[0]
    hbm = pl.BlockSpec(memory_space=pltpu.HBM)
    vmem = pl.BlockSpec(memory_space=pltpu.VMEM)
    return pl.pallas_call(
        output_kernel,
        out_shape=jax.ShapeDtypeStruct((width, ROWS), jnp.bfloat16),
        in_specs=[vmem] * 5,
        out_specs=hbm,
        scratch_shapes=[
            pltpu.VMEM((ROWS, HD), jnp.bfloat16),
            pltpu.VMEM((width, ROWS), jnp.bfloat16),
            pltpu.SemaphoreType.DMA((2,)),
        ],
        compiler_params=pltpu.CompilerParams(vmem_limit_bytes=40 << 20),
        cost_estimate=pl.CostEstimate(
            flops=2 * ROWS * HD * (width + 4 * LANES),
            bytes_accessed=2 * (2 * ROWS * HD + HD * width + ROWS * width),
            transcendentals=0,
        ),
        name="guided_columns",
    )(own_queries, other_queries, own_states, other_states, weight)


def comes_before(axis, mask):
    index = lax.axis_index(axis)
    return ((index ^ mask) < index).astype(jnp.float32)


def row_source(mask, j):
    x = lax.axis_index(X)
    return (lax.axis_index(TM) - x + (x ^ mask)) * FR + j


def reached_part(first, mask, both, second):
    one = (first <= row_source(mask, 1)).astype(jnp.float32)
    two = (first <= row_source(mask, 0)).astype(jnp.float32)
    return both.astype(jnp.float32) * two + second.astype(jnp.float32) * (one - two)


def window_kernel(first_ref, total1, total2, total3, second1, second2, second3, frames, out_ref):
    others = tuple(zip(MASKS, (total1, total2, total3), (second1, second2, second3), strict=True))
    for i in range(FR):
        first = first_ref[i]
        value = reached_part(first, 0, frames[0] + frames[1], frames[1])
        for mask, both, second in others:
            value = value + reached_part(first, mask, both[...], second[...])
        out_ref[i] = (value * (first != 0).astype(jnp.float32)).astype(jnp.bfloat16)


def early_kernel(first_ref, *refs):
    parts, refs = refs[: len(EARLY)], refs[len(EARLY) :]
    totals, seconds, (window, frames, out_ref) = refs[:3], refs[3:6], refs[6:]
    prefix = None
    for part, (axis, mask) in zip(parts, EARLY, strict=True):
        term = part[...].astype(jnp.float32) * comes_before(axis, mask)
        prefix = term if prefix is None else prefix + term
    later_row = (lax.axis_index(ROW) > 0).astype(jnp.float32)
    for i in range(FR):
        first = first_ref[i]
        value = prefix * (first == 0).astype(jnp.float32)
        value = value + window[i].astype(jnp.float32) * later_row
        for mask, both, second in zip(MASKS, totals, seconds, strict=True):
            part = reached_part(first, mask, both[...], second[...])
            value = value + part * comes_before(X, mask)
        for j in range(i + 1):
            value = value + frames[j] * (first <= row_source(0, j)).astype(jnp.float32)
        out_ref[i] = value


def late_kernel(first_ref, base_ref, *refs):
    *parts, out_ref = refs
    prefix = None
    for part, (axis, mask) in zip(parts, LATE, strict=True):
        term = part[...].astype(jnp.float32) * comes_before(axis, mask)
        prefix = term if prefix is None else prefix + term
    own_scale = jnp.where(lax.axis_index("cfg") == 0, guide_scale, 1.0 - guide_scale)
    for i in range(FR):
        whole = (first_ref[i] == 0).astype(jnp.float32)
        value = base_ref[i] + prefix * whole
        out_ref[i, :, :HD] = (value[:, :HD] * own_scale).astype(jnp.bfloat16)
        out_ref[i, :, HD:] = value[:, HD:].astype(jnp.bfloat16)


def small_call(kernel, dtype, name, first_frame, *arrays):
    return pl.pallas_call(
        kernel,
        out_shape=jax.ShapeDtypeStruct((FR, DH, PACKED), dtype),
        in_specs=[pl.BlockSpec(memory_space=pltpu.SMEM)]
        + [pl.BlockSpec(memory_space=pltpu.VMEM)] * len(arrays),
        out_specs=pl.BlockSpec(memory_space=pltpu.VMEM),
        compiler_params=pltpu.CompilerParams(vmem_limit_bytes=4 << 20),
        cost_estimate=pl.CostEstimate(
            flops=4 * DH * PACKED * len(arrays),
            bytes_accessed=4 * DH * PACKED * len(arrays),
            transcendentals=0,
        ),
        name=name,
    )(first_frame, *arrays)


def exchanged(value, axis, mask):
    pairs = [(i, i ^ mask) for i in range(lax.axis_size(axis))]
    return lax.ppermute(value, axis, pairs)


def shifted(value, axis, steps):
    count = lax.axis_size(axis)
    return lax.ppermute(value, axis, [(i, (i + steps) % count) for i in range(count)])


def summed(total, arrived):
    return sum((a.astype(jnp.float32) for a in arrived), total.astype(jnp.float32)).astype(
        jnp.bfloat16
    )


def on_device(queries, key_vectors, value_vectors, out_weight, first_frame):
    own_queries = queries[0]
    other_queries = exchanged(own_queries, "cfg", 1)
    next_first = shifted(first_frame, ROW, -1)
    frames, total, second = frame_states(key_vectors[0], value_vectors[0])

    parts_x = [exchanged(total, X, m) for m in MASKS]
    total = summed(total, parts_x)
    total, other_queries, next_first = lax.optimization_barrier((total, other_queries, next_first))
    seconds = [exchanged(second, X, m) for m in MASKS]
    parts_z = [exchanged(total, Z, m) for m in (1, 2, 3)]
    window = small_call(
        window_kernel, jnp.bfloat16, "window_mix", next_first, *parts_x, *seconds, frames
    )
    window = shifted(window, ROW, 1)
    total = summed(total, parts_z)
    parts_w = [exchanged(total, Z, 7)]
    total = summed(total, parts_w)
    total, later_weight = lax.optimization_barrier((total, out_weight.T))
    half_weight = fetched(later_weight)
    parts_y = [exchanged(total, Y, m) for m in (1, 2, 3)]

    early = (*parts_z, *parts_w, *parts_x, *seconds, window, frames)
    base = small_call(early_kernel, jnp.float32, "early_mix", first_frame, *early)
    base, half_weight = lax.optimization_barrier((base, half_weight))
    own_states = small_call(late_kernel, jnp.bfloat16, "late_mix", first_frame, base, *parts_y)
    other_states = exchanged(own_states, "cfg", 1)
    return guided_columns(
        own_queries, other_queries, own_states, other_states, half_weight
    ).T


def solution(mesh):
    torus = Mesh(mesh.devices.reshape(mesh.shape["cfg"], 4, 8, 4), ("cfg", "tm_0", "tm_1", "tm_2"))
    in_specs = (P("cfg", TM, None), P("cfg", TM, None), P("cfg", TM, None), P(), P(TM))
    return jax.shard_map(
        on_device, mesh=torus, in_specs=in_specs, out_specs=P(TM, "cfg"), check_vma=False
    )
```

```python
import jax
import jax.numpy as jnp
from jax import lax
from jax.experimental import pallas as pl
from jax.experimental.pallas import tpu as pltpu
from jax.sharding import Mesh
from jax.sharding import PartitionSpec as P

H = 36
DH = 32
FR = 2
FT = 384
HD = H * DH
LANES = 128
BLOCKS = HD // LANES
HEADS_PER_BLOCK = LANES // DH
PACKED = HD + LANES
ROWS = FR * FT
TM = ("tm_0", "tm_1", "tm_2")
Y, Z, X = TM
ROW = (Y, Z)
MASKS = (1, 2, 3)
EARLY = ((Z, 1), (Z, 2), (Z, 3), (Z, 7))
LATE = ((Y, 1), (Y, 2), (Y, 3))
VMEM_LIMIT = 16 << 20

guide_scale = 4.5
epsilon = 1e-06


def state_kernel(k_hbm, v_hbm, frames_ref, total_ref, second_ref, k_buf, v_buf, sems):
    def copies(f):
        rows = pl.ds(f * FT, FT)
        return (
            pltpu.make_async_copy(k_hbm.at[rows], k_buf.at[rows], sems.at[0, f]),
            pltpu.make_async_copy(v_hbm.at[rows], v_buf.at[rows], sems.at[1, f]),
        )

    for f in range(FR):
        for copy in copies(f):
            copy.start()
    lane = lax.broadcasted_iota(jnp.int32, (DH, LANES), 1)
    ones = jnp.ones((FT, LANES), jnp.bfloat16)
    for f in range(FR):
        rows = slice(f * FT, (f + 1) * FT)
        for copy in copies(f):
            copy.wait()
        sums = jnp.zeros((DH, LANES), jnp.float32)
        for b in range(BLOCKS):
            columns = slice(b * LANES, (b + 1) * LANES)
            keys = jnp.maximum(k_buf[rows, columns], 0)
            both = jnp.concatenate([v_buf[rows, columns], ones], axis=1)
            outer = lax.dot_general(
                keys, both, (((0,), (0,)), ((), ())), preferred_element_type=jnp.float32
            )
            state = jnp.zeros((DH, LANES), jnp.float32)
            for h in range(HEADS_PER_BLOCK):
                piece = outer[h * DH : (h + 1) * DH]
                state = jnp.where(lane // DH == h, piece[:, :LANES], state)
                sums = jnp.where(lane == b * HEADS_PER_BLOCK + h, piece[:, LANES:], sums)
            frames_ref[f, :, columns] = state
        frames_ref[f, :, HD:] = sums
    second = frames_ref[FR - 1]
    second_ref[...] = second.astype(jnp.bfloat16)
    total_ref[...] = (frames_ref[0] + second).astype(jnp.bfloat16)


def in_hbm(value):
    return pltpu.with_memory_space_constraint(value, pltpu.HBM)


def frame_states(keys, values):
    return pl.pallas_call(
        state_kernel,
        out_shape=(
            jax.ShapeDtypeStruct((FR, DH, PACKED), jnp.float32),
            jax.ShapeDtypeStruct((DH, PACKED), jnp.bfloat16),
            jax.ShapeDtypeStruct((DH, PACKED), jnp.bfloat16),
        ),
        in_specs=[pl.BlockSpec(memory_space=pltpu.HBM)] * 2,
        out_specs=(pl.BlockSpec(memory_space=pltpu.VMEM),) * 3,
        scratch_shapes=[
            pltpu.VMEM((ROWS, HD), jnp.bfloat16),
            pltpu.VMEM((ROWS, HD), jnp.bfloat16),
            pltpu.SemaphoreType.DMA((2, FR)),
        ],
        compiler_params=pltpu.CompilerParams(vmem_limit_bytes=VMEM_LIMIT),
        cost_estimate=pl.CostEstimate(
            flops=2 * ROWS * HD * 2 * LANES, bytes_accessed=4 * ROWS * HD, transcendentals=0
        ),
        name="frame_states",
    )(in_hbm(keys), in_hbm(values))


def attend(q_ref, s_ref, emit):
    head = lax.broadcasted_iota(jnp.int32, (LANES, HD), 0)
    lane = lax.broadcasted_iota(jnp.int32, (LANES, HD), 1)
    spread = (head == lane // DH).astype(jnp.bfloat16)
    row_of = lax.broadcasted_iota(jnp.int32, (LANES, LANES), 0) // DH
    lane_of = lax.broadcasted_iota(jnp.int32, (LANES, LANES), 1) // DH
    own_head = (row_of == lane_of).astype(jnp.bfloat16)
    for f in range(FR):
        rows = slice(f * FT, (f + 1) * FT)
        sums = jnp.dot(s_ref[f, :, HD:], spread, preferred_element_type=jnp.float32)
        sums = sums.astype(jnp.bfloat16)
        for b in range(BLOCKS):
            columns = slice(b * LANES, (b + 1) * LANES)
            state = jnp.concatenate([s_ref[f, :, columns]] * HEADS_PER_BLOCK, axis=0)
            total = jnp.concatenate([sums[:, columns]] * HEADS_PER_BLOCK, axis=0)
            both = jnp.concatenate([state * own_head, total * own_head], axis=1)
            feats = jnp.maximum(q_ref[rows, columns], 0)
            part = jnp.dot(feats, both, preferred_element_type=jnp.float32)
            emit(rows, columns, part[:, :LANES] / (part[:, LANES:] + epsilon))


def own_kernel(q_ref, s_ref, own_ref):
    def emit(rows, columns, attended):
        own_ref[rows, columns] = attended

    attend(q_ref, s_ref, emit)


def own_branch(queries, states):
    return pl.pallas_call(
        own_kernel,
        out_shape=jax.ShapeDtypeStruct((ROWS, HD), jnp.float32),
        in_specs=[pl.BlockSpec(memory_space=pltpu.VMEM)] * 2,
        out_specs=pl.BlockSpec(memory_space=pltpu.VMEM),
        compiler_params=pltpu.CompilerParams(vmem_limit_bytes=VMEM_LIMIT),
        cost_estimate=pl.CostEstimate(
            flops=4 * ROWS * HD * LANES, bytes_accessed=6 * ROWS * HD, transcendentals=0
        ),
        name="own_branch",
    )(queries, states)


def output_kernel(own_ref, q_ref, s_ref, w_ref, out_hbm, x_buf, out_buf, out_sems):
    width = out_hbm.shape[0]
    part = width // 2

    def out_copy(c):
        rows = pl.ds(c * part, part)
        return pltpu.make_async_copy(out_buf.at[rows], out_hbm.at[rows], out_sems.at[c])

    def emit(rows, columns, attended):
        x_buf[rows, columns] = (own_ref[rows, columns] + attended).astype(jnp.bfloat16)

    attend(q_ref, s_ref, emit)
    for c in range(2):
        rows = slice(c * part, (c + 1) * part)
        out_buf[rows, :] = lax.dot_general(
            w_ref[rows, :], x_buf[...], (((1,), (1,)), ((), ())), preferred_element_type=jnp.float32
        ).astype(jnp.bfloat16)
        out_copy(c).start()
    for c in range(2):
        out_copy(c).wait()


def fetch_kernel(w_hbm, w_ref, sem):
    width = w_ref.shape[0]
    start = pl.multiple_of(lax.axis_index("cfg") * width, 16)
    copy = pltpu.make_async_copy(w_hbm.at[pl.ds(start, width)], w_ref, sem)
    copy.start()
    copy.wait()


def fetched(weight):
    width = weight.shape[0] // 2
    return pl.pallas_call(
        fetch_kernel,
        out_shape=jax.ShapeDtypeStruct((width, weight.shape[1]), weight.dtype),
        in_specs=[pl.BlockSpec(memory_space=pltpu.HBM)],
        out_specs=pl.BlockSpec(memory_space=pltpu.VMEM),
        scratch_shapes=[pltpu.SemaphoreType.DMA],
        compiler_params=pltpu.CompilerParams(vmem_limit_bytes=2 << 20),
        cost_estimate=pl.CostEstimate(
            flops=0, bytes_accessed=2 * weight.size, transcendentals=0
        ),
        name="fetch",
    )(in_hbm(weight))


def guided_columns(own, other_queries, other_states, weight):
    width = weight.shape[0]
    hbm = pl.BlockSpec(memory_space=pltpu.HBM)
    vmem = pl.BlockSpec(memory_space=pltpu.VMEM)
    return pl.pallas_call(
        output_kernel,
        out_shape=jax.ShapeDtypeStruct((width, ROWS), jnp.bfloat16),
        in_specs=[vmem] * 4,
        out_specs=hbm,
        scratch_shapes=[
            pltpu.VMEM((ROWS, HD), jnp.bfloat16),
            pltpu.VMEM((width, ROWS), jnp.bfloat16),
            pltpu.SemaphoreType.DMA((2,)),
        ],
        compiler_params=pltpu.CompilerParams(vmem_limit_bytes=40 << 20),
        cost_estimate=pl.CostEstimate(
            flops=2 * ROWS * HD * (width + 4 * LANES),
            bytes_accessed=2 * (2 * ROWS * HD + HD * width + ROWS * width),
            transcendentals=0,
        ),
        name="guided_columns",
    )(own, other_queries, other_states, weight)


def comes_before(axis, mask):
    index = lax.axis_index(axis)
    return ((index ^ mask) < index).astype(jnp.float32)


def row_source(mask, j):
    x = lax.axis_index(X)
    return (lax.axis_index(TM) - x + (x ^ mask)) * FR + j


def reached_part(first, mask, both, second):
    one = (first <= row_source(mask, 1)).astype(jnp.float32)
    two = (first <= row_source(mask, 0)).astype(jnp.float32)
    return both.astype(jnp.float32) * two + second.astype(jnp.float32) * (one - two)


def window_kernel(first_ref, total1, total2, total3, second1, second2, second3, frames, out_ref):
    others = tuple(zip(MASKS, (total1, total2, total3), (second1, second2, second3), strict=True))
    for i in range(FR):
        first = first_ref[i]
        value = reached_part(first, 0, frames[0] + frames[1], frames[1])
        for mask, both, second in others:
            value = value + reached_part(first, mask, both[...], second[...])
        out_ref[i] = (value * (first != 0).astype(jnp.float32)).astype(jnp.bfloat16)


def early_kernel(first_ref, *refs):
    parts, refs = refs[: len(EARLY)], refs[len(EARLY) :]
    totals, seconds, (window, frames, out_ref) = refs[:3], refs[3:6], refs[6:]
    prefix = None
    for part, (axis, mask) in zip(parts, EARLY, strict=True):
        term = part[...].astype(jnp.float32) * comes_before(axis, mask)
        prefix = term if prefix is None else prefix + term
    later_row = (lax.axis_index(ROW) > 0).astype(jnp.float32)
    for i in range(FR):
        first = first_ref[i]
        value = prefix * (first == 0).astype(jnp.float32)
        value = value + window[i].astype(jnp.float32) * later_row
        for mask, both, second in zip(MASKS, totals, seconds, strict=True):
            part = reached_part(first, mask, both[...], second[...])
            value = value + part * comes_before(X, mask)
        for j in range(i + 1):
            value = value + frames[j] * (first <= row_source(0, j)).astype(jnp.float32)
        out_ref[i] = value


def late_kernel(first_ref, base_ref, *refs):
    *parts, out_ref = refs
    prefix = None
    for part, (axis, mask) in zip(parts, LATE, strict=True):
        term = part[...].astype(jnp.float32) * comes_before(axis, mask)
        prefix = term if prefix is None else prefix + term
    own_scale = jnp.where(lax.axis_index("cfg") == 0, guide_scale, 1.0 - guide_scale)
    for i in range(FR):
        whole = (first_ref[i] == 0).astype(jnp.float32)
        value = base_ref[i] + prefix * whole
        out_ref[i, :, :HD] = (value[:, :HD] * own_scale).astype(jnp.bfloat16)
        out_ref[i, :, HD:] = value[:, HD:].astype(jnp.bfloat16)


def small_call(kernel, dtype, name, first_frame, *arrays):
    return pl.pallas_call(
        kernel,
        out_shape=jax.ShapeDtypeStruct((FR, DH, PACKED), dtype),
        in_specs=[pl.BlockSpec(memory_space=pltpu.SMEM)]
        + [pl.BlockSpec(memory_space=pltpu.VMEM)] * len(arrays),
        out_specs=pl.BlockSpec(memory_space=pltpu.VMEM),
        compiler_params=pltpu.CompilerParams(vmem_limit_bytes=4 << 20),
        cost_estimate=pl.CostEstimate(
            flops=4 * DH * PACKED * len(arrays),
            bytes_accessed=4 * DH * PACKED * len(arrays),
            transcendentals=0,
        ),
        name=name,
    )(first_frame, *arrays)


def exchanged(value, axis, mask):
    pairs = [(i, i ^ mask) for i in range(lax.axis_size(axis))]
    return lax.ppermute(value, axis, pairs)


def shifted(value, axis, steps):
    count = lax.axis_size(axis)
    return lax.ppermute(value, axis, [(i, (i + steps) % count) for i in range(count)])


def summed(total, arrived):
    return sum((a.astype(jnp.float32) for a in arrived), total.astype(jnp.float32)).astype(
        jnp.bfloat16
    )


def on_device(queries, key_vectors, value_vectors, out_weight, first_frame):
    own_queries = queries[0]
    other_queries = exchanged(own_queries, "cfg", 1)
    next_first = shifted(first_frame, ROW, -1)
    frames, total, second = frame_states(key_vectors[0], value_vectors[0])

    parts_x = [exchanged(total, X, m) for m in MASKS]
    total = summed(total, parts_x)
    total, other_queries, next_first = lax.optimization_barrier((total, other_queries, next_first))
    seconds = [exchanged(second, X, m) for m in MASKS]
    parts_z = [exchanged(total, Z, m) for m in (1, 2, 3)]
    window = small_call(
        window_kernel, jnp.bfloat16, "window_mix", next_first, *parts_x, *seconds, frames
    )
    window = shifted(window, ROW, 1)
    total = summed(total, parts_z)
    parts_w = [exchanged(total, Z, 7)]
    total = summed(total, parts_w)
    total, later_weight = lax.optimization_barrier((total, out_weight.T))
    half_weight = fetched(later_weight)
    parts_y = [exchanged(total, Y, m) for m in (1, 2, 3)]

    early = (*parts_z, *parts_w, *parts_x, *seconds, window, frames)
    base = small_call(early_kernel, jnp.float32, "early_mix", first_frame, *early)
    base, half_weight = lax.optimization_barrier((base, half_weight))
    own_states = small_call(late_kernel, jnp.bfloat16, "late_mix", first_frame, base, *parts_y)
    other_states = exchanged(own_states, "cfg", 1)
    own = own_branch(own_queries, own_states)
    return guided_columns(own, other_queries, other_states, half_weight).T


def solution(mesh):
    torus = Mesh(mesh.devices.reshape(mesh.shape["cfg"], 4, 8, 4), ("cfg", "tm_0", "tm_1", "tm_2"))
    in_specs = (P("cfg", TM, None), P("cfg", TM, None), P("cfg", TM, None), P(), P(TM))
    return jax.shard_map(
        on_device, mesh=torus, in_specs=in_specs, out_specs=P(TM, "cfg"), check_vma=False
    )
```
